256 devices in a mesh: front: 8 (over x, core), grp: 32 (over y, z).
Axes of the slice: x: 4, y: 4, z: 8, core: 2. Of those that a mesh axis runs over, the one named last changes fastest.
Arguments:
- panel_block: bfloat16 [8, 4608, 1024], P('front', 'grp'), may hold values from -0.1796875 to 0.1796875
- trailing: float32 [8, 4608, 4608], P('front', 'grp')
- inverse: float32 [8, 1024, 1024], P('front')
- weights: float32 [8, 4608], P('front'), may hold values from -0.09375 to 0.09375
- live_size: int32 [8], P('front'), may hold values from 2304 to 4608, as said below
- column_source: int32 [8, 4608], P('front'), may hold values from 0 to 4607, each once within a row
- destination: int32 [8, 4608, 1], P('front', 'grp'), may hold values from 0 to 7; in each aligned block of 144 rows (0 to 143, 144 to 287, ..., all dimensions but the last counted through in order) at most 36 rows name the same one
- row_offset: int32 [8, 4608], P('front', 'grp'), may hold values from 0 to 143
Outputs:
- factor: float32 [8, 4608, 1024], P('front', 'grp')
- checksum: float32 [8, 4608], P('front', 'grp')
- ancestor: float32 [8, 4608, 4608], P('front', 'grp')
The draws below stay inside these ranges and needn't reach their ends.
Inputs may be any that keep to these rules, and one draw needn't show every extreme that they name: `live_size`: each front's live size is 4608 minus a multiple of 576; one front is full. `destination`: among the 144 rows of one device at most 36 rows name the same ancestor front. `column_source`: each front's row is a permutation.
All inputs are finite; a program needn't handle non-finite values.
Results may differ from the reference program's by a relative error of at most 0.0003.
Values may be sent and summed in bfloat16 or wider, within the bound.
A program may use at most 128 MiB of HBM per device.

```python
import math
import jax
import jax.numpy as jnp
import numpy as np
from jax import lax

M = 4608
P_SIZE = 1024
NF = 8
ROWS_DEV = 144
CAP = 36


def draw_trailing(key, part):
    first, second = jax.random.split(key)
    base = jax.random.normal(first, (NF, M, M), jnp.float32) * 0.7
    symmetric = 0.5 * (base + jnp.swapaxes(base, 1, 2))
    diagonal = jax.random.uniform(second, (NF, M), jnp.float32, 3.0, 5.0)
    return symmetric + diagonal[:, :, None] * jnp.eye(M, dtype=jnp.float32)[None]


def draw_inverse(key, part):
    first, second = jax.random.split(key)
    lower = jax.random.normal(first, (NF, P_SIZE, P_SIZE), jnp.float32) * (0.8 / P_SIZE ** 0.5)
    lower = jnp.tril(lower, -1)
    diagonal = jax.random.uniform(second, (NF, P_SIZE), jnp.float32, 1.0, 2.0)
    return lower + diagonal[:, :, None] * jnp.eye(P_SIZE, dtype=jnp.float32)[None]


def draw_live_size(key, part):
    first, second = jax.random.split(key)
    drawn_steps = jax.random.randint(first, (NF,), 0, 5)
    order = jax.random.permutation(second, NF)
    drawn_steps = jnp.where(order == 0, 0, jnp.where(order == 1, 4, drawn_steps))
    return (M - M // 8 * drawn_steps).astype(jnp.int32)


def touch_ends(values, key, least, largest):
    place = [jax.random.randint(jax.random.fold_in(key, axis), (), 0, length) for axis, length in enumerate(values.shape)]
    widest = values.shape.index(max(values.shape))
    beside = place[:widest] + [(place[widest] + 1) % values.shape[widest]] + place[widest + 1:]
    return values.at[tuple(place)].set(least).at[tuple(beside)].set(largest)


def block_scale(own_key, shape, shards, least, top_value):
    factor_of, own = 1.0, jax.random.fold_in(own_key, 6)
    for position, parts in shards:
        steps = jnp.exp(jax.random.uniform(jax.random.fold_in(own, position), (parts,), jnp.float32, least / len(shards), top_value / len(shards)))
        factor_of = factor_of * jnp.repeat(steps, shape[position] // parts).reshape([-1 if axis == position else 1 for axis in range(len(shape))])
    return factor_of


def deal_out(key, own, number, rows, number_of, top, limit, slope):
    ranking = jax.random.permutation(key, number_of)
    packed, ordinary = portions_of(number_of, rows * top, limit, slope, True), portions_of(number_of, rows * top, limit, slope, False)
    places = jnp.arange(number_of)

    def named(tallies, turn):
        used = int((tallies > 0).sum())
        fixed = max(1, used // 4)
        passed = fixed + (places - fixed + turn * (used - fixed)) % max(1, number_of - fixed)
        return jnp.zeros((number_of,), jnp.int32).at[ranking[jnp.where(places < fixed, places, passed)]].set(jnp.asarray(tallies, jnp.int32))

    tallies = jnp.where(number % 4 == 0, named(packed, number // 4), named(ordinary, number - number // 4 - 1))
    mixed = jax.random.permutation(jax.random.fold_in(own, 3), number_of)
    donor, taker = mixed[0:number_of // 2 * 2:2], mixed[1:number_of // 2 * 2:2]
    margin = jnp.minimum(tallies[donor] - 1, limit - tallies[taker]) // 2
    margin = jnp.where((donor == ranking[0]) | (taker == ranking[0]) | (tallies[taker] == 0), 0, jnp.maximum(margin, 0))
    passed = jax.random.randint(jax.random.fold_in(own, 4), (number_of // 2,), 0, 1 << 20) % (margin + 1)
    tallies = tallies.at[donor].add(-passed).at[taker].add(passed)
    members = jnp.searchsorted(jnp.cumsum(tallies), jnp.arange(rows * top), side="right").astype(jnp.int32)
    grid = members.reshape(top, rows).T
    grid = grid[jax.random.permutation(jax.random.fold_in(own, 1), rows)]
    turn = jax.random.randint(jax.random.fold_in(own, 2), (rows, 1), 0, top)
    return jnp.take_along_axis(grid, (jnp.arange(top)[None, :] + turn) % top, axis=1)


def portions_of(count, total, limit, lean, full):
    weights = [(1 << 20) // math.isqrt(grade ** lean) + 1 for grade in range(1, count + 1)]
    largest = limit if full else min(limit, max(-(-total // count), total * weights[0] // sum(weights)))
    least = 1 if total - largest >= count - 1 else 0
    given, spare = [largest] + [least] * (count - 1), total - largest - least * (count - 1)
    while spare > 0:
        candidates = [i for i in range(1, count) if given[i] < largest] or [i for i in range(1, count) if given[i] < limit]
        pool, left = sum([weights[i] for i in candidates]), spare
        for i in candidates:
            more = min(limit - given[i], max(1, left * weights[i] // pool), spare)
            given[i] = given[i] + more
            spare = spare - more
    return np.array(given)


def normal_values(own_key, dims, width, bound, cuts=(), kind=jnp.bfloat16):
    level = block_scale(own_key, dims, cuts, -0.22, 0.18) if cuts else 1.0
    result = jax.random.normal(own_key, dims, jnp.float32) * width * level
    return jnp.minimum(jnp.maximum(result, -bound), bound).astype(kind)


def setup_inputs(seed: int = 0) -> dict:
    streams_of = jax.random.split(jax.random.key(seed), 9)
    panel_block = normal_values(streams_of[0], (NF, M, P_SIZE), 0.03, 0.1796875, ((0, 8), (1, 32)))
    trailing = draw_trailing(jax.random.fold_in(streams_of[8], 71), 0)
    inverse = draw_inverse(jax.random.fold_in(streams_of[8], 71), 0)
    weights = normal_values(streams_of[3], (NF, M), M ** -0.5, 0.09375, ((0, 8),), jnp.float32)
    live_size = draw_live_size(jax.random.fold_in(streams_of[8], 71), 0)
    column_source = jax.vmap(lambda own: jax.random.permutation(own, M))(jax.random.split(streams_of[5], NF)).reshape((NF, M)).astype(jnp.int32)
    destination_keys = jax.random.split(jax.random.fold_in(streams_of[6], 1), NF * M // ROWS_DEV)
    destination_turns = jax.random.permutation(jax.random.fold_in(streams_of[6], 3), NF * M // ROWS_DEV)
    destination = jax.vmap(lambda own, number: deal_out(jax.random.fold_in(streams_of[6], 2), own, number, ROWS_DEV, NF, 1, CAP, 2))(destination_keys, destination_turns).reshape((NF, M, 1))
    row_offset = touch_ends(jax.random.randint(streams_of[7], (NF, M), 0, ROWS_DEV), jax.random.fold_in(streams_of[7], 1), 0, ROWS_DEV - 1).astype(jnp.int32)
    return {"panel_block": panel_block, "trailing": trailing, "inverse": inverse, "weights": weights, "live_size": live_size, "column_source": column_source, "destination": destination, "row_offset": row_offset}


def reference(panel_block, trailing, inverse, weights, live_size, column_source, destination, row_offset):
    highest_precision = lax.Precision.HIGHEST
    positions = jnp.arange(M, dtype=jnp.int32)

    def one_front(ancestor, inputs):
        panel_rows, trail_rows, inverse_rows, weight_rows, live_count, source, dest_front, offsets = inputs
        factor = jnp.dot(panel_rows.astype(jnp.float32), inverse_rows.T, precision=highest_precision)
        schur_rows = trail_rows - jnp.dot(factor, factor.T, precision=highest_precision)
        colmask = (positions < live_count).astype(jnp.float32)
        checksum = jnp.dot(schur_rows, weight_rows * colmask, precision=highest_precision)
        keep_cols = (source < live_count).astype(jnp.float32)
        permuted = jnp.take(schur_rows, source, axis=1) * keep_cols[None, :]
        target_front = jnp.where(positions < live_count, dest_front[:, 0], NF).astype(jnp.int32)
        target_row = ((positions // ROWS_DEV) * ROWS_DEV + offsets).astype(jnp.int32)
        ancestor = ancestor.at[target_front, target_row].add(permuted, mode="drop")
        return ancestor, (factor, checksum)

    initial = jnp.zeros((NF, M, M), jnp.float32)
    ancestor, outputs = lax.scan(one_front, initial, (panel_block, trailing, inverse, weights, live_size, column_source, destination, row_offset))
    return outputs[0], outputs[1], ancestor
```

```python
import jax
import jax.numpy as jnp
from jax import lax
from jax.sharding import PartitionSpec as P

HIGHEST = lax.Precision.HIGHEST


def bf16_terms(x):
    high = lax.reduce_precision(x, 8, 7)
    rest = x - high
    middle = lax.reduce_precision(rest, 8, 7)
    low = rest - middle
    return [t.astype(jnp.bfloat16) for t in (high, middle, low)]


def on_device(
    panel_block, trailing, inverse, weights, live_size, column_source, destination, row_offset
):
    row_count = trailing.shape[1]
    col_count = trailing.shape[2]
    fronts = lax.axis_size("front")
    capacity = max(2, 2 * row_count // fronts)
    slots = fronts * capacity
    trail_rows = trailing[0]
    inverse_rows = inverse[0]
    live_count = live_size[0]
    panel_all = lax.all_gather(panel_block[0], "grp", axis=0, tiled=True)
    panel_f32 = panel_block[0].astype(jnp.float32)
    factor = jnp.dot(panel_f32, inverse_rows.T, precision=HIGHEST)
    twice = jnp.dot(factor, inverse_rows, precision=HIGHEST)

    rows = jnp.arange(row_count, dtype=jnp.int32)
    live_rows = lax.axis_index("grp") * row_count + rows < live_count
    dest_front = jnp.where(live_rows, destination[0, :, 0], -1)
    earlier = (dest_front[:, None] == dest_front[None, :]) & (rows[None, :] < rows[:, None])
    slot_index = jnp.sum(earlier.astype(jnp.int32), axis=1)
    flat_slot = jnp.where(live_rows, dest_front * capacity + slot_index, -1)
    place = flat_slot[None, :] == jnp.arange(slots, dtype=jnp.int32)[:, None]
    row_tags = jnp.sum(jnp.where(place, row_offset[0][None, :] + 1, 0), axis=1) - 1
    row_tags = row_tags.astype(jnp.float32).reshape(fronts, capacity)
    received_tags = lax.all_to_all(row_tags, "front", split_axis=0, concat_axis=0, tiled=True)
    targets = received_tags.reshape(slots).astype(jnp.int32)
    land = (targets[None, :] == rows[:, None]).astype(jnp.float32)

    source = column_source[0]
    keep = (source < live_count).astype(jnp.float32)
    trail_permuted = jnp.take(trail_rows, source, axis=1)
    kept_weights = jnp.take(weights[0], source) * keep

    update = sum(
        lax.dot_general(
            term, panel_all, (((1,), (1,)), ((), ())), preferred_element_type=jnp.float32
        )
        for term in bf16_terms(twice)
    )
    permuted = (trail_permuted - jnp.take(update, source, axis=1)) * keep[None, :]
    checksum = jnp.dot(permuted, kept_weights, precision=HIGHEST)
    bucket = jnp.dot(place.astype(jnp.float32), permuted, precision=HIGHEST)
    received = lax.all_to_all(
        bucket.reshape(fronts, capacity, col_count), "front", split_axis=0, concat_axis=0, tiled=True
    )
    ancestor = jnp.dot(land, received.reshape(slots, col_count), precision=HIGHEST)
    return (factor[None], checksum[None], ancestor[None])


def solution(mesh):
    placed = (
        P("front", "grp", None),
        P("front", "grp", None),
        P("front", None, None),
        P("front", None),
        P("front"),
        P("front", None),
        P("front", "grp", None),
        P("front", "grp"),
    )
    return jax.shard_map(
        on_device,
        mesh=mesh,
        in_specs=placed,
        out_specs=(P("front", "grp", None), P("front", "grp"), P("front", "grp", None)),
        check_vma=False,
    )
```

```python
import jax
import jax.numpy as jnp
from jax import lax
from jax.sharding import PartitionSpec as P

HIGHEST = lax.Precision.HIGHEST
PANEL_TOP = 0.1796875


def bf16_terms(x):
    high = lax.reduce_precision(x, 8, 7)
    rest = x - high
    middle = lax.reduce_precision(rest, 8, 7)
    low = rest - middle
    return [t.astype(jnp.bfloat16) for t in (high, middle, low)]


def dot_bf16(a, b):
    return jnp.dot(a, b, preferred_element_type=jnp.float32)


def on_device(
    panel_block, trailing, inverse, weights, live_size, column_source, destination, row_offset
):
    row_count = trailing.shape[1]
    col_count = trailing.shape[2]
    fronts = lax.axis_size("front")
    capacity = -(-(row_count // 4) // 8) * 8
    slots = fronts * capacity
    trail_rows = trailing[0]
    inverse_rows = inverse[0]
    live_count = live_size[0]
    source = column_source[0]
    panel_all = lax.all_gather(panel_block[0], "grp", axis=0, tiled=True)
    panel_f32 = panel_block[0].astype(jnp.float32)
    factor = jnp.dot(panel_f32, inverse_rows.T, precision=HIGHEST)
    twice = jnp.dot(factor, inverse_rows, precision=HIGHEST)

    bound = jnp.max(jnp.abs(trail_rows), axis=1) + PANEL_TOP * jnp.sum(jnp.abs(twice), axis=1)
    scale = lax.reduce_precision(jnp.clip(bound, 2.0**-100, 2.0**120), 8, 0)
    inverse_scale = lax.reduce_precision(1.0 / scale, 8, 0)

    rows = jnp.arange(row_count, dtype=jnp.int32)
    live_rows = lax.axis_index("grp") * row_count + rows < live_count
    dest_front = jnp.where(live_rows, destination[0, :, 0], -1)
    earlier = (dest_front[:, None] == dest_front[None, :]) & (rows[None, :] < rows[:, None])
    slot_index = jnp.sum(earlier.astype(jnp.int32), axis=1)
    flat_slot = jnp.where(live_rows, dest_front * capacity + slot_index, -1)
    place = flat_slot[None, :] == jnp.arange(slots, dtype=jnp.int32)[:, None]
    row_tags = jnp.sum(jnp.where(place, row_offset[0][None, :] + 1, 0), axis=1) - 1
    row_tags = row_tags.astype(jnp.float32).reshape(fronts, 1, capacity)
    row_scales = jnp.sum(jnp.where(place, scale[None, :], 0.0), axis=1).reshape(fronts, 1, capacity)
    received_tags = lax.all_to_all(
        jnp.concatenate([row_tags, row_scales], axis=1),
        "front", split_axis=0, concat_axis=0, tiled=True,
    )
    targets = received_tags[:, 0].reshape(slots).astype(jnp.int32)
    scales = received_tags[:, 1].reshape(slots)
    land = jnp.where(targets[None, :] == rows[:, None], scales[None, :], 0.0).astype(jnp.bfloat16)
    spread = jnp.where(place, inverse_scale[None, :], 0.0).astype(jnp.bfloat16)

    columns = jnp.arange(col_count, dtype=jnp.int32)
    keep = source < live_count
    masked_weights = jnp.where(columns < live_count, weights[0], 0.0)
    trail_permuted = jnp.take(trail_rows, source, axis=1)
    weight_terms = jnp.stack(bf16_terms(masked_weights))
    trail_sum = jnp.sum(trail_rows * masked_weights[None, :], axis=1)

    terms = jnp.concatenate(bf16_terms(twice)[:2], axis=0)
    panel_all, factor, twice, terms, trail_permuted, trail_sum, land, spread = (
        lax.optimization_barrier(
            (panel_all, factor, twice, terms, trail_permuted, trail_sum, land, spread)
        )
    )
    panel_permuted = jnp.take(panel_all, source, axis=0)
    update = lax.dot_general(
        terms, panel_permuted, (((1,), (1,)), ((), ())), preferred_element_type=jnp.float32
    )
    update = update[:row_count] + update[row_count:]
    permuted = jnp.where(keep[None, :], trail_permuted - update, 0.0)
    high, middle, _ = bf16_terms(permuted)
    bucket = (dot_bf16(spread, high) + dot_bf16(spread, middle)).astype(jnp.float16)
    bucket, panel_all = lax.optimization_barrier((bucket, panel_all))
    received = lax.all_to_all(
        bucket.reshape(fronts, capacity, col_count), "front", split_axis=0, concat_axis=0, tiled=True
    )
    weighted = jnp.sum(dot_bf16(weight_terms, panel_all), axis=0)
    checksum = trail_sum - jnp.sum(twice * weighted, axis=1)
    received = received.reshape(slots, col_count).astype(jnp.float32)
    high, middle, _ = bf16_terms(received)
    ancestor = dot_bf16(land, high) + dot_bf16(land, middle)
    return (factor[None], checksum[None], ancestor[None])


def solution(mesh):
    placed = (
        P("front", "grp", None),
        P("front", "grp", None),
        P("front", None, None),
        P("front", None),
        P("front"),
        P("front", None),
        P("front", "grp", None),
        P("front", "grp"),
    )
    return jax.shard_map(
        on_device,
        mesh=mesh,
        in_specs=placed,
        out_specs=(P("front", "grp", None), P("front", "grp"), P("front", "grp", None)),
        check_vma=False,
    )
```

```python
import functools
import heapq

import jax
import jax.numpy as jnp
from jax import lax
from jax.experimental import pallas as pl
from jax.experimental.pallas import tpu as pltpu
from jax.sharding import PartitionSpec as P

HIGHEST = lax.Precision.HIGHEST
PANEL_TOP = 0.1796875


def bf16_terms(x):
    high = lax.reduce_precision(x, 8, 7)
    rest = x - high
    middle = lax.reduce_precision(rest, 8, 7)
    low = rest - middle
    return [t.astype(jnp.bfloat16) for t in (high, middle, low)]


RINGS = (4, 8)
SHARES = ((1, 0, 0, 5), (0, 1, 5, 8))


def gather_plan():
    copies, steps, free, heap = [], [], {}, []
    landed = {}

    def send(now, share, phase, offset, hop, way):
        axis = SHARES[share][phase]
        span = SHARES[share][3] - SHARES[share][2]
        size = span / 8 * (0.5 if hop == RINGS[axis] // 2 else 1.0)
        link = (axis, way)
        free[link] = max(now, free.get(link, 0.0)) + 6.3 * size
        heapq.heappush(heap, (free[link] + 1.6, len(copies)))
        copies.append((share, phase, offset, hop, way))

    def forward(now, share, phase, offset, hop):
        for way in (1, -1):
            send(now, share, phase, offset, hop, way)

    for phase in (0, 1):
        for share in (0, 1):
            forward(0.0, share, phase, 0, 1)
    starts = len(copies)
    while heap:
        now, number = heapq.heappop(heap)
        share, phase, offset, hop, way = copies[number]
        half = RINGS[SHARES[share][phase]] // 2
        first = len(copies)
        if hop < half:
            send(now, share, phase, offset, hop + 1, way)
        if phase == 0:
            place = -way * hop if hop < half else half
            landed[share, place] = landed.get((share, place), 0) + 1
            if hop < half or landed[share, place] == 2:
                forward(now, share, 1, place, 1)
        steps.append((number, range(first, len(copies))))
    return copies, starts, steps


def gather_kernel(plan, panel_ref, all_ref, send_sems, recv_sems, own_sem):
    copies, starts, steps = plan
    rows, width = panel_ref.shape
    cut = rows * 5 // 9
    me = lax.axis_index("grp")
    here = (me // RINGS[1], me % RINGS[1])

    def neighbour(axis, way):
        there = list(here)
        there[axis] = (here[axis] + way + RINGS[axis]) % RINGS[axis]
        return {"grp": there[0] * RINGS[1] + there[1]}

    def copy_of(number, arriving):
        share, phase, offset, hop, way = copies[number]
        first, second, begin, end = SHARES[share]
        axis = SHARES[share][phase]
        moved = -way * (hop if arriving else hop - 1)
        spot = [None, None]
        spot[first] = moved if phase == 0 else offset
        spot[second] = 0 if phase == 0 else moved
        own = spot == [0, 0]
        spot = [(h + o + n) % n for h, o, n in zip(here, spot, RINGS)]
        if hop < RINGS[axis] // 2:
            part = pl.ds(0, rows)
        else:
            part = pl.ds(0, cut) if way == 1 else pl.ds(cut, rows - cut)
        columns = pl.ds(begin * width // 8, (end - begin) * width // 8)
        target = all_ref.at[spot[0], spot[1], part, columns]
        return pltpu.make_async_remote_copy(
            src_ref=panel_ref.at[part, columns] if own else target,
            dst_ref=target,
            send_sem=send_sems.at[number],
            recv_sem=recv_sems.at[number],
            device_id=neighbour(axis, way),
            device_id_type=pl.DeviceIdType.MESH,
        )

    barrier = pltpu.get_barrier_semaphore()
    for axis in (0, 1):
        for way in (1, -1):
            pl.semaphore_signal(
                barrier, inc=1, device_id=neighbour(axis, way), device_id_type=pl.DeviceIdType.MESH
            )
    pl.semaphore_wait(barrier, 4)

    for number in range(starts):
        copy_of(number, False).start()
    keep = pltpu.make_async_copy(panel_ref, all_ref.at[here[0], here[1]], own_sem)
    keep.start()
    for number, following in steps:
        copy_of(number, True).wait_recv()
        for later in following:
            copy_of(later, False).start()
    keep.wait()
    for number in range(len(copies)):
        copy_of(number, False).wait_send()


def gather_panels(panel):
    plan = gather_plan()
    count = len(plan[0])
    rows, width = panel.shape
    gathered = pl.pallas_call(
        functools.partial(gather_kernel, plan),
        out_shape=jax.ShapeDtypeStruct((*RINGS, rows, width), panel.dtype),
        in_specs=[pl.BlockSpec(memory_space=pltpu.VMEM)],
        out_specs=pl.BlockSpec(memory_space=pl.ANY),
        scratch_shapes=[
            pltpu.SemaphoreType.DMA((count,)),
            pltpu.SemaphoreType.DMA((count,)),
            pltpu.SemaphoreType.DMA,
        ],
        compiler_params=pltpu.CompilerParams(collective_id=0, has_side_effects=True),
    )(panel)
    return gathered.reshape(RINGS[0] * RINGS[1] * rows, width)


def dot_bf16(a, b):
    return jnp.dot(a, b, preferred_element_type=jnp.float32)


def on_device(
    panel_block, trailing, inverse, weights, live_size, column_source, destination, row_offset
):
    row_count = trailing.shape[1]
    col_count = trailing.shape[2]
    fronts = lax.axis_size("front")
    capacity = -(-(row_count // 4) // 8) * 8
    slots = fronts * capacity
    trail_rows = trailing[0]
    inverse_rows = inverse[0]
    live_count = live_size[0]
    source = column_source[0]
    panel_all = gather_panels(panel_block[0])
    panel_f32 = panel_block[0].astype(jnp.float32)
    factor = jnp.dot(panel_f32, inverse_rows.T, precision=HIGHEST)
    twice = jnp.dot(factor, inverse_rows, precision=HIGHEST)

    bound = jnp.max(jnp.abs(trail_rows), axis=1) + PANEL_TOP * jnp.sum(jnp.abs(twice), axis=1)
    scale = lax.reduce_precision(jnp.clip(bound, 2.0**-100, 2.0**120), 8, 0)
    inverse_scale = lax.reduce_precision(1.0 / scale, 8, 0)

    rows = jnp.arange(row_count, dtype=jnp.int32)
    live_rows = lax.axis_index("grp") * row_count + rows < live_count
    dest_front = jnp.where(live_rows, destination[0, :, 0], -1)
    earlier = (dest_front[:, None] == dest_front[None, :]) & (rows[None, :] < rows[:, None])
    slot_index = jnp.sum(earlier.astype(jnp.int32), axis=1)
    flat_slot = jnp.where(live_rows, dest_front * capacity + slot_index, -1)
    place = flat_slot[None, :] == jnp.arange(slots, dtype=jnp.int32)[:, None]
    row_tags = jnp.sum(jnp.where(place, row_offset[0][None, :] + 1, 0), axis=1) - 1
    row_tags = row_tags.astype(jnp.float32).reshape(fronts, 1, capacity)
    row_scales = jnp.sum(jnp.where(place, scale[None, :], 0.0), axis=1).reshape(fronts, 1, capacity)
    received_tags = lax.all_to_all(
        jnp.concatenate([row_tags, row_scales], axis=1),
        "front", split_axis=0, concat_axis=0, tiled=True,
    )
    targets = received_tags[:, 0].reshape(slots).astype(jnp.int32)
    scales = received_tags[:, 1].reshape(slots)
    land = jnp.where(targets[None, :] == rows[:, None], scales[None, :], 0.0).astype(jnp.bfloat16)
    spread = jnp.where(place, inverse_scale[None, :], 0.0).astype(jnp.bfloat16)

    columns = jnp.arange(col_count, dtype=jnp.int32)
    keep = source < live_count
    masked_weights = jnp.where(columns < live_count, weights[0], 0.0)

    terms = jnp.concatenate(bf16_terms(twice)[:2], axis=0)
    update = lax.dot_general(
        terms, panel_all, (((1,), (1,)), ((), ())), preferred_element_type=jnp.float32
    )
    schur = trail_rows - (update[:row_count] + update[row_count:])
    permuted = jnp.where(keep[None, :], jnp.take(schur, source, axis=1), 0.0)
    high, middle, _ = bf16_terms(permuted)
    bucket = (dot_bf16(spread, high) + dot_bf16(spread, middle)).astype(jnp.float16)
    bucket, schur = lax.optimization_barrier((bucket, schur))
    received = lax.all_to_all(
        bucket.reshape(fronts, capacity, col_count), "front", split_axis=0, concat_axis=0, tiled=True
    )
    checksum = jnp.sum(schur * masked_weights[None, :], axis=1)
    received = received.reshape(slots, col_count).astype(jnp.float32)
    high, middle, _ = bf16_terms(received)
    ancestor = dot_bf16(land, high) + dot_bf16(land, middle)
    return (factor[None], checksum[None], ancestor[None])


def solution(mesh):
    placed = (
        P("front", "grp", None),
        P("front", "grp", None),
        P("front", None, None),
        P("front", None),
        P("front"),
        P("front", None),
        P("front", "grp", None),
        P("front", "grp"),
    )
    return jax.shard_map(
        on_device,
        mesh=mesh,
        in_specs=placed,
        out_specs=(P("front", "grp", None), P("front", "grp"), P("front", "grp", None)),
        check_vma=False,
    )
```

```python
import functools
import heapq

import jax
import jax.numpy as jnp
from jax import lax
from jax.experimental import pallas as pl
from jax.experimental.pallas import tpu as pltpu
from jax.sharding import PartitionSpec as P

HIGHEST = lax.Precision.HIGHEST
PANEL_TOP = 0.1796875
LANES = 128
CHUNKS = 2


def bf16_terms(x):
    high = lax.reduce_precision(x, 8, 7)
    rest = x - high
    middle = lax.reduce_precision(rest, 8, 7)
    low = rest - middle
    return [t.astype(jnp.bfloat16) for t in (high, middle, low)]


RINGS = (4, 8)
SHARES = ((1, 0, 0, 5), (0, 1, 5, 8))


def gather_plan():
    copies, steps, free, heap = [], [], {}, []
    landed = {}

    def send(now, share, phase, offset, hop, way):
        axis = SHARES[share][phase]
        span = SHARES[share][3] - SHARES[share][2]
        size = span / 8 * (0.5 if hop == RINGS[axis] // 2 else 1.0)
        link = (axis, way)
        free[link] = max(now, free.get(link, 0.0)) + 6.3 * size
        heapq.heappush(heap, (free[link] + 1.6, len(copies)))
        copies.append((share, phase, offset, hop, way))

    def forward(now, share, phase, offset, hop):
        for way in (1, -1):
            send(now, share, phase, offset, hop, way)

    for phase in (0, 1):
        for share in (0, 1):
            forward(0.0, share, phase, 0, 1)
    starts = len(copies)
    while heap:
        now, number = heapq.heappop(heap)
        share, phase, offset, hop, way = copies[number]
        half = RINGS[SHARES[share][phase]] // 2
        first = len(copies)
        if hop < half:
            send(now, share, phase, offset, hop + 1, way)
        if phase == 0:
            place = -way * hop if hop < half else half
            landed[share, place] = landed.get((share, place), 0) + 1
            if hop < half or landed[share, place] == 2:
                forward(now, share, 1, place, 1)
        steps.append((number, range(first, len(copies))))
    return copies, starts, steps


def gather_kernel(plan, panel_ref, all_ref, send_sems, recv_sems, own_sem):
    copies, starts, steps = plan
    rows, width = panel_ref.shape
    cut = rows * 5 // 9
    me = lax.axis_index("grp")
    here = (me // RINGS[1], me % RINGS[1])

    def neighbour(axis, way):
        there = list(here)
        there[axis] = (here[axis] + way + RINGS[axis]) % RINGS[axis]
        return {"grp": there[0] * RINGS[1] + there[1]}

    def copy_of(number, arriving):
        share, phase, offset, hop, way = copies[number]
        first, second, begin, end = SHARES[share]
        axis = SHARES[share][phase]
        moved = -way * (hop if arriving else hop - 1)
        spot = [None, None]
        spot[first] = moved if phase == 0 else offset
        spot[second] = 0 if phase == 0 else moved
        own = spot == [0, 0]
        spot = [(h + o + n) % n for h, o, n in zip(here, spot, RINGS)]
        if hop < RINGS[axis] // 2:
            part = pl.ds(0, rows)
        else:
            part = pl.ds(0, cut) if way == 1 else pl.ds(cut, rows - cut)
        columns = pl.ds(begin * width // 8, (end - begin) * width // 8)
        target = all_ref.at[spot[0], spot[1], part, columns]
        return pltpu.make_async_remote_copy(
            src_ref=panel_ref.at[part, columns] if own else target,
            dst_ref=target,
            send_sem=send_sems.at[number],
            recv_sem=recv_sems.at[number],
            device_id=neighbour(axis, way),
            device_id_type=pl.DeviceIdType.MESH,
        )

    barrier = pltpu.get_barrier_semaphore()
    for axis in (0, 1):
        for way in (1, -1):
            pl.semaphore_signal(
                barrier, inc=1, device_id=neighbour(axis, way), device_id_type=pl.DeviceIdType.MESH
            )
    pl.semaphore_wait(barrier, 4)

    for number in range(starts):
        copy_of(number, False).start()
    keep = pltpu.make_async_copy(panel_ref, all_ref.at[here[0], here[1]], own_sem)
    keep.start()
    for number, following in steps:
        copy_of(number, True).wait_recv()
        for later in following:
            copy_of(later, False).start()
    keep.wait()
    for number in range(len(copies)):
        copy_of(number, False).wait_send()


def gather_panels(panel):
    plan = gather_plan()
    count = len(plan[0])
    rows, width = panel.shape
    gathered = pl.pallas_call(
        functools.partial(gather_kernel, plan),
        out_shape=jax.ShapeDtypeStruct((*RINGS, rows, width), panel.dtype),
        in_specs=[pl.BlockSpec(memory_space=pltpu.VMEM)],
        out_specs=pl.BlockSpec(memory_space=pl.ANY),
        scratch_shapes=[
            pltpu.SemaphoreType.DMA((count,)),
            pltpu.SemaphoreType.DMA((count,)),
            pltpu.SemaphoreType.DMA,
        ],
        compiler_params=pltpu.CompilerParams(collective_id=0, has_side_effects=True),
    )(panel)
    return gathered.reshape(RINGS[0] * RINGS[1] * rows, width)


def dot_bf16(a, b):
    return jnp.dot(a, b, preferred_element_type=jnp.float32)


def on_device(
    panel_block, trailing, inverse, weights, live_size, column_source, destination, row_offset
):
    row_count = trailing.shape[1]
    col_count = trailing.shape[2]
    fronts = lax.axis_size("front")
    used = row_count // 4
    capacity = -(-(used + 2) // 8) * 8
    slots = fronts * capacity
    trail_rows = trailing[0]
    inverse_rows = inverse[0]
    live_count = live_size[0]
    source = column_source[0]
    panel_all = gather_panels(panel_block[0])
    panel_f32 = panel_block[0].astype(jnp.float32)
    factor = jnp.dot(panel_f32, inverse_rows.T, precision=HIGHEST)
    twice = jnp.dot(factor, inverse_rows, precision=HIGHEST)

    bound = jnp.max(jnp.abs(trail_rows), axis=1) + PANEL_TOP * jnp.sum(jnp.abs(twice), axis=1)
    scale = lax.reduce_precision(jnp.clip(bound, 2.0**-100, 2.0**120), 8, 0)
    inverse_scale = lax.reduce_precision(1.0 / scale, 8, 0)

    rows = jnp.arange(row_count, dtype=jnp.int32)
    live_rows = lax.axis_index("grp") * row_count + rows < live_count
    dest_front = jnp.where(live_rows, destination[0, :, 0], -1)
    earlier = (dest_front[:, None] == dest_front[None, :]) & (rows[None, :] < rows[:, None])
    slot_index = jnp.sum(earlier.astype(jnp.int32), axis=1)
    flat_slot = jnp.where(live_rows, dest_front * capacity + slot_index, -1)
    place = flat_slot[None, :] == jnp.arange(slots, dtype=jnp.int32)[:, None]
    slot_tags = jnp.sum(jnp.where(place, row_offset[0][None, :] + 1, 0), axis=1) - 1
    exponents = jnp.round(jnp.log2(scale))
    slot_exponents = jnp.sum(jnp.where(place, exponents[None, :], 0.0), axis=1)
    tags = jnp.zeros((fronts, capacity, LANES), jnp.float32)
    tags = tags.at[:, used, :capacity].set(slot_tags.astype(jnp.float32).reshape(fronts, capacity))
    tags = tags.at[:, used + 1, :capacity].set(slot_exponents.reshape(fronts, capacity))
    tags = tags.reshape(slots, LANES)
    spread = jnp.where(place, inverse_scale[None, :], 0.0).astype(jnp.bfloat16)

    columns = jnp.arange(col_count, dtype=jnp.int32)
    keep = source < live_count
    masked_weights = jnp.where(columns < live_count, weights[0], 0.0)

    terms = jnp.concatenate(bf16_terms(twice)[:2], axis=0)
    update = lax.dot_general(
        terms, panel_all, (((1,), (1,)), ((), ())), preferred_element_type=jnp.float32
    )
    schur = trail_rows - (update[:row_count] + update[row_count:])
    width = col_count // CHUNKS
    received = []
    for chunk in range(CHUNKS):
        part = slice(chunk * width, (chunk + 1) * width)
        permuted = jnp.where(keep[None, part], jnp.take(schur, source[part], axis=1), 0.0)
        high, middle, _ = bf16_terms(permuted)
        bucket = dot_bf16(spread, high) + dot_bf16(spread, middle)
        if chunk == 0:
            bucket = bucket + jnp.pad(tags, ((0, 0), (0, width - LANES)))
        bucket = bucket.astype(jnp.float16)
        bucket, source, masked_weights = lax.optimization_barrier((bucket, source, masked_weights))
        received.append(
            lax.all_to_all(
                bucket.reshape(fronts, capacity, width),
                "front", split_axis=0, concat_axis=0, tiled=True,
            )
        )
    checksum = jnp.sum(schur * masked_weights[None, :], axis=1)

    heads = received[0][:, used : used + 2, :capacity].astype(jnp.float32)
    targets = heads[:, 0].reshape(slots).astype(jnp.int32)
    scales = lax.reduce_precision(jnp.exp2(heads[:, 1].reshape(slots)), 8, 0)
    land = jnp.where(targets[None, :] == rows[:, None], scales[None, :], 0.0).astype(jnp.bfloat16)
    ancestor = []
    for block in received:
        high, middle, _ = bf16_terms(block.reshape(slots, width).astype(jnp.float32))
        ancestor.append(dot_bf16(land, high) + dot_bf16(land, middle))
    ancestor = jnp.concatenate(ancestor, axis=1)
    return (factor[None], checksum[None], ancestor[None])


def solution(mesh):
    placed = (
        P("front", "grp", None),
        P("front", "grp", None),
        P("front", None, None),
        P("front", None),
        P("front"),
        P("front", None),
        P("front", "grp", None),
        P("front", "grp"),
    )
    return jax.shard_map(
        on_device,
        mesh=mesh,
        in_specs=placed,
        out_specs=(P("front", "grp", None), P("front", "grp"), P("front", "grp", None)),
        check_vma=False,
    )
```

```python
import functools
import heapq

import jax
import jax.numpy as jnp
from jax import lax
from jax.experimental import pallas as pl
from jax.experimental.pallas import tpu as pltpu
from jax.sharding import PartitionSpec as P

HIGHEST = lax.Precision.HIGHEST
PANEL_TOP = 0.1796875
LANES = 128


def bf16_terms(x):
    high = lax.reduce_precision(x, 8, 7)
    rest = x - high
    middle = lax.reduce_precision(rest, 8, 7)
    low = rest - middle
    return [t.astype(jnp.bfloat16) for t in (high, middle, low)]


RINGS = (4, 8)
SHARES = ((1, 0, 0, 5), (0, 1, 5, 8))


def gather_plan():
    copies, steps, free, heap = [], [], {}, []
    landed = {}

    def send(now, share, phase, offset, hop, way):
        axis = SHARES[share][phase]
        span = SHARES[share][3] - SHARES[share][2]
        size = span / 8 * (0.5 if hop == RINGS[axis] // 2 else 1.0)
        link = (axis, way)
        free[link] = max(now, free.get(link, 0.0)) + 6.3 * size
        heapq.heappush(heap, (free[link] + 1.6, len(copies)))
        copies.append((share, phase, offset, hop, way))

    def forward(now, share, phase, offset, hop):
        for way in (1, -1):
            send(now, share, phase, offset, hop, way)

    for phase in (0, 1):
        for share in (0, 1):
            forward(0.0, share, phase, 0, 1)
    starts = len(copies)
    while heap:
        now, number = heapq.heappop(heap)
        share, phase, offset, hop, way = copies[number]
        half = RINGS[SHARES[share][phase]] // 2
        first = len(copies)
        if hop < half:
            send(now, share, phase, offset, hop + 1, way)
        if phase == 0:
            place = -way * hop if hop < half else half
            landed[share, place] = landed.get((share, place), 0) + 1
            if hop < half or landed[share, place] == 2:
                forward(now, share, 1, place, 1)
        steps.append((number, range(first, len(copies))))
    return copies, starts, steps


def gather_kernel(plan, panel_ref, all_ref, send_sems, recv_sems, own_sem):
    copies, starts, steps = plan
    rows, width = panel_ref.shape
    cut = rows * 5 // 9
    me = lax.axis_index("grp")
    here = (me // RINGS[1], me % RINGS[1])

    def neighbour(axis, way):
        there = list(here)
        there[axis] = (here[axis] + way + RINGS[axis]) % RINGS[axis]
        return {"grp": there[0] * RINGS[1] + there[1]}

    def copy_of(number, arriving):
        share, phase, offset, hop, way = copies[number]
        first, second, begin, end = SHARES[share]
        axis = SHARES[share][phase]
        moved = -way * (hop if arriving else hop - 1)
        spot = [None, None]
        spot[first] = moved if phase == 0 else offset
        spot[second] = 0 if phase == 0 else moved
        own = spot == [0, 0]
        spot = [(h + o + n) % n for h, o, n in zip(here, spot, RINGS)]
        if hop < RINGS[axis] // 2:
            part = pl.ds(0, rows)
        else:
            part = pl.ds(0, cut) if way == 1 else pl.ds(cut, rows - cut)
        columns = pl.ds(begin * width // 8, (end - begin) * width // 8)
        target = all_ref.at[spot[0], spot[1], part, columns]
        return pltpu.make_async_remote_copy(
            src_ref=panel_ref.at[part, columns] if own else target,
            dst_ref=target,
            send_sem=send_sems.at[number],
            recv_sem=recv_sems.at[number],
            device_id=neighbour(axis, way),
            device_id_type=pl.DeviceIdType.MESH,
        )

    barrier = pltpu.get_barrier_semaphore()
    for axis in (0, 1):
        for way in (1, -1):
            pl.semaphore_signal(
                barrier, inc=1, device_id=neighbour(axis, way), device_id_type=pl.DeviceIdType.MESH
            )
    pl.semaphore_wait(barrier, 4)

    for number in range(starts):
        copy_of(number, False).start()
    keep = pltpu.make_async_copy(panel_ref, all_ref.at[here[0], here[1]], own_sem)
    keep.start()
    for number, following in steps:
        copy_of(number, True).wait_recv()
        for later in following:
            copy_of(later, False).start()
    keep.wait()
    for number in range(len(copies)):
        copy_of(number, False).wait_send()


def gather_panels(panel):
    plan = gather_plan()
    count = len(plan[0])
    rows, width = panel.shape
    gathered = pl.pallas_call(
        functools.partial(gather_kernel, plan),
        out_shape=jax.ShapeDtypeStruct((*RINGS, rows, width), panel.dtype),
        in_specs=[pl.BlockSpec(memory_space=pltpu.VMEM)],
        out_specs=pl.BlockSpec(memory_space=pl.ANY),
        scratch_shapes=[
            pltpu.SemaphoreType.DMA((count,)),
            pltpu.SemaphoreType.DMA((count,)),
            pltpu.SemaphoreType.DMA,
        ],
        compiler_params=pltpu.CompilerParams(collective_id=0, has_side_effects=True),
    )(panel)
    return gathered.reshape(RINGS[0] * RINGS[1] * rows, width)


def on_device(
    panel_block, trailing, inverse, weights, live_size, column_source, destination, row_offset
):
    row_count = trailing.shape[1]
    col_count = trailing.shape[2]
    fronts = lax.axis_size("front")
    used = row_count // 4
    capacity = -(-(used + 2) // 8) * 8
    slots = fronts * capacity
    trail_rows = trailing[0]
    inverse_rows = inverse[0]
    live_count = live_size[0]
    source = column_source[0]
    panel_all = gather_panels(panel_block[0])
    panel_f32 = panel_block[0].astype(jnp.float32)
    factor = jnp.dot(panel_f32, inverse_rows.T, precision=HIGHEST)
    twice = jnp.dot(factor, inverse_rows, precision=HIGHEST)

    bound = jnp.max(jnp.abs(trail_rows), axis=1) + PANEL_TOP * jnp.sum(jnp.abs(twice), axis=1)
    scale = lax.reduce_precision(jnp.clip(bound, 2.0**-100, 2.0**120), 8, 0)
    inverse_scale = lax.reduce_precision(1.0 / scale, 8, 0)

    rows = jnp.arange(row_count, dtype=jnp.int32)
    live_rows = lax.axis_index("grp") * row_count + rows < live_count
    dest_front = jnp.where(live_rows, destination[0, :, 0], -1)
    earlier = (dest_front[:, None] == dest_front[None, :]) & (rows[None, :] < rows[:, None])
    slot_index = jnp.sum(earlier.astype(jnp.int32), axis=1)
    flat_slot = jnp.where(live_rows, dest_front * capacity + slot_index, -1)
    place = flat_slot[None, :] == jnp.arange(slots, dtype=jnp.int32)[:, None]
    slot_tags = jnp.sum(jnp.where(place, row_offset[0][None, :] + 1, 0), axis=1) - 1
    exponents = jnp.round(jnp.log2(scale))
    slot_exponents = jnp.sum(jnp.where(place, exponents[None, :], 0.0), axis=1)
    tags = jnp.zeros((fronts, capacity, LANES), jnp.float32)
    tags = tags.at[:, used, :capacity].set(slot_tags.astype(jnp.float32).reshape(fronts, capacity))
    tags = tags.at[:, used + 1, :capacity].set(slot_exponents.reshape(fronts, capacity))
    tags = tags.reshape(slots, LANES)
    spread = jnp.where(place, inverse_scale[None, :], 0.0)

    columns = jnp.arange(col_count, dtype=jnp.int32)
    keep = source < live_count
    masked_weights = jnp.where(columns < live_count, weights[0], 0.0)

    terms = jnp.concatenate(bf16_terms(twice)[:2], axis=0)
    update = lax.dot_general(
        terms, panel_all, (((1,), (1,)), ((), ())), preferred_element_type=jnp.float32
    )
    schur = trail_rows - (update[:row_count] + update[row_count:])
    early = col_count * 2 // 5 // LANES * LANES
    received = []
    for begin, end in ((0, early), (early, col_count)):
        part = slice(begin, end)
        width = end - begin
        permuted = jnp.where(keep[None, part], jnp.take(schur, source[part], axis=1), 0.0)
        bucket = jnp.dot(spread, permuted, precision=lax.Precision.HIGH)
        if begin == 0:
            bucket = bucket + jnp.pad(tags, ((0, 0), (0, width - LANES)))
        bucket = bucket.astype(jnp.float16)
        bucket, source, masked_weights = lax.optimization_barrier((bucket, source, masked_weights))
        received.append(
            lax.all_to_all(
                bucket.reshape(fronts, capacity, width),
                "front", split_axis=0, concat_axis=0, tiled=True,
            )
        )
    checksum = jnp.sum(schur * masked_weights[None, :], axis=1)

    heads = received[0][:, used : used + 2, :capacity].astype(jnp.float32)
    targets = heads[:, 0].reshape(slots).astype(jnp.int32)
    scales = lax.reduce_precision(jnp.exp2(heads[:, 1].reshape(slots)), 8, 0)
    land = jnp.where(targets[None, :] == rows[:, None], scales[None, :], 0.0)
    ancestor = []
    for block in received:
        block = block.reshape(slots, -1).astype(jnp.float32)
        ancestor.append(jnp.dot(land, block, precision=lax.Precision.HIGH))
    ancestor = jnp.concatenate(ancestor, axis=1)
    return (factor[None], checksum[None], ancestor[None])


def solution(mesh):
    placed = (
        P("front", "grp", None),
        P("front", "grp", None),
        P("front", None, None),
        P("front", None),
        P("front"),
        P("front", None),
        P("front", "grp", None),
        P("front", "grp"),
    )
    return jax.shard_map(
        on_device,
        mesh=mesh,
        in_specs=placed,
        out_specs=(P("front", "grp", None), P("front", "grp"), P("front", "grp", None)),
        check_vma=False,
    )
```
